128 devices in a mesh: tm: 8 (over x_hi, z), chan: 16 (over y, x_lo, core).
Axes of the slice: x: 4 (x_hi: 2, x_lo: 2; x = x_hi * 2 + x_lo), y: 4, z: 4, core: 2. Of those that a mesh axis runs over, the one named last changes fastest.
Arguments:
- raw_data: float32 [10240, 6144], P('tm', 'chan'), may hold values from -6 to 6
- fir_taps: float32 [33], replicated, may hold values from -1 to 1
- spectral_weight: float32 [64], replicated, may hold values from 0.1 to 1
Outputs:
- correlations: float32 [128, 201, 10240], P('chan', None, 'tm')
The draws below stay inside these ranges and needn't reach their ends.
All inputs are finite; a program needn't handle non-finite values.
Results may differ from the reference program's by a relative error of at most 0.0034.
Values may be sent and summed in bfloat16 or wider, within the bound.
A program may use at most 192 MiB of HBM per device.

```python
import jax
import jax.numpy as jnp
from jax import lax

C = 10240
HK = 16
TN = 64
SEG = 128
HALF = 100
S = 6144
SRCS = 128
LAGS = 201
KT = 33
NB = 64


def levels(own_key, dims, split, smallest, top_value):
    loudness, own = 1.0, jax.random.fold_in(own_key, 6)
    for position, parts in split:
        heights = jnp.exp(jax.random.uniform(jax.random.fold_in(own, position), (parts,), jnp.float32, smallest / len(split), top_value / len(split)))
        loudness = loudness * jnp.repeat(heights, dims[position] // parts).reshape([-1 if axis == position else 1 for axis in range(len(dims))])
    return loudness


def noise(own_key, extent, spread, bound, split=(), kind=jnp.bfloat16):
    array = spread * jax.random.normal(own_key, extent, jnp.float32)
    if split:
        array = array * levels(own_key, extent, split, -0.22, 0.18)
    return jnp.clip(array, -bound, bound).astype(kind)


def setup_inputs(seed: int = 0) -> dict:
    key_list = jax.random.split(jax.random.key(seed), 4)
    return {
        "raw_data": noise(key_list[0], (C, S), 1.0, 6.0, ((0, 8), (1, 16)), jnp.float32),
        "fir_taps": noise(key_list[1], (KT,), KT ** -0.5, 1.0, (), jnp.float32),
        "spectral_weight": jnp.clip(jax.random.uniform(key_list[2], (NB,), jnp.float32, 0.1, 1.0), 0.1, 1.0),
    }


EPS = 1e-06
FLOOR = 0.5
HIGHEST = lax.Precision.HIGHEST

def dft_tables(seg_len):
    bin_count = seg_len // 2
    time_idx = jnp.arange(seg_len, dtype=jnp.int32)
    freq_idx = jnp.arange(bin_count, dtype=jnp.int32)
    product_mod = time_idx[:, None] * freq_idx[None, :] % seg_len
    phase_angle = 2.0 * jnp.pi / seg_len * product_mod.astype(jnp.float32)
    forward = jnp.concatenate([jnp.cos(phase_angle), jnp.sin(phase_angle)], axis=1)
    weight = jnp.where(freq_idx == 0, 1.0, 2.0).astype(jnp.float32)
    inverse = jnp.concatenate([jnp.cos(phase_angle).T * weight[:, None], jnp.sin(phase_angle).T * weight[:, None]], axis=0)
    return (forward, inverse / jnp.sqrt(jnp.float32(seg_len)))

def whiten(segments, spectral_weight, forward, inverse):
    bin_count = forward.shape[1] // 2
    spectrum = jnp.dot(segments, forward, precision=HIGHEST)
    cos_part = spectrum[:, :bin_count]
    sin_part = spectrum[:, bin_count:]
    amplitude = jnp.sqrt(cos_part * cos_part + sin_part * sin_part)
    mean_amplitude = lax.optimization_barrier(jnp.mean(amplitude, axis=1, keepdims=True)) + EPS
    bin_scale = spectral_weight[None, :] / jnp.maximum(amplitude, FLOOR * mean_amplitude)
    scaled = jnp.concatenate([cos_part * bin_scale, sin_part * bin_scale], axis=1)
    return jnp.dot(scaled, inverse, precision=HIGHEST)

def lag_stack(sources, sample_total):
    count = sources.shape[0]
    padded = jnp.pad(sources, ((0, 0), (HALF, HALF + 1)))
    width = padded.shape[1]
    repeated = jnp.broadcast_to(padded[:, None, :], (count, LAGS, width)).reshape(count, LAGS * width)
    shifted = repeated[:, :LAGS * (width - 1)].reshape(count, LAGS, width - 1)
    return shifted[:, :, 2 * HALF:2 * HALF + sample_total]

def reference(raw_data, fir_taps, spectral_weight):
    chan_total, samples = raw_data.shape
    padded = jnp.pad(raw_data, ((0, 0), (HK, HK)))
    filtered = jnp.zeros_like(raw_data)
    for tap_index in range(KT):
        filtered = filtered + fir_taps[tap_index] * padded[:, tap_index:tap_index + samples]
    window = 2 * TN + 1
    magnitude = jnp.abs(filtered)
    summed = lax.reduce_window(magnitude, jnp.zeros((), magnitude.dtype), lax.add, (1, window), (1, 1), ((0, 0), (TN, TN)))
    normalized = filtered / (summed / window + EPS)
    forward, inverse = dft_tables(SEG)
    forward = forward.astype(raw_data.dtype)
    inverse = inverse.astype(raw_data.dtype)
    whitened = whiten(normalized.reshape(chan_total * samples // SEG, SEG), spectral_weight, forward, inverse)
    whitened = whitened.reshape(chan_total, samples).astype(jnp.bfloat16)
    sources = whitened[::C // SRCS]
    receivers_t = whitened.astype(jnp.float32).T

    def one_source(source_row):
        lagged = lag_stack(source_row[None, :], samples)[0]
        return jnp.dot(lagged.astype(jnp.float32), receivers_t)
    result = lax.map(one_source, sources)
    return result * samples ** (-0.5)
```

```python
import functools

import jax
import jax.numpy as jnp
import ml_dtypes
import numpy as np
from jax import lax
from jax.experimental import pallas as pl
from jax.experimental.pallas import tpu as pltpu
from jax.sharding import PartitionSpec as P

HK = 16
TN = 64
SEG = 128
HALF = 100
LAGS = 201
LPAD = 208
EPS = 1e-06
FLOOR = 0.5
HALO = HK + TN
BF = jnp.bfloat16
F32 = jnp.float32


def split_np(table):
    table = np.asarray(table, np.float32)
    hi = table.astype(ml_dtypes.bfloat16)
    lo = (table - hi.astype(np.float32)).astype(ml_dtypes.bfloat16)
    return hi, lo


def tables():
    t, f = np.arange(SEG), np.arange(SEG // 2)
    angle = 2.0 * np.pi * ((t[:, None] * f[None, :]) % SEG) / SEG
    forward = np.concatenate([np.cos(angle), np.sin(angle)], axis=1)
    weight = np.where(f == 0, 1.0, 2.0)[:, None]
    inverse = np.concatenate([np.cos(angle).T * weight, np.sin(angle).T * weight]) / np.sqrt(SEG)
    stacked = []
    for table in (forward, inverse):
        row = np.concatenate(split_np(table), axis=1)
        stacked.append(np.concatenate([row, row], axis=0))
    i, o = np.arange(384)[:, None], np.arange(256)[None, :]
    band = ((i - o >= 0) & (i - o <= 2 * TN)).astype(ml_dtypes.bfloat16)
    mean = np.full((256, 128), 1.0 / 128, ml_dtypes.bfloat16)
    return stacked[0], stacked[1], band, mean


def dot(a, b):
    return jnp.dot(a, b, preferred_element_type=F32)


def split2(x):
    hi = x.astype(BF)
    return hi, (x - hi.astype(F32)).astype(BF)


def split3(x):
    hi = x.astype(BF)
    rest = x - hi.astype(F32)
    mid = rest.astype(BF)
    return hi, mid, (rest - mid.astype(F32)).astype(BF)


def front_kernel(raw, left, right, toep, weight, fwd, inv, band, mean, out, ext, t_hi, t_mid, t_lo):
    chan = lax.axis_index("chan")
    ends = lax.axis_size("chan") - 1

    @pl.when(pl.program_id(0) == 0)
    def _():
        hi, mid, lo = split3(toep[...])
        t_hi[...] = hi
        t_mid[...] = mid
        t_lo[...] = lo

    n = raw.shape[1]
    ext[:, 0:HALO] = left[...]
    ext[:, HALO : HALO + n] = raw[...]
    ext[:, HALO + n : 2 * HALO + n] = right[...]
    ext[:, 2 * HALO + n :] = jnp.zeros((ext.shape[0], ext.shape[1] - 2 * HALO - n), F32)

    def fir(x):
        hi, mid, lo = split3(x)
        small = dot(mid, t_mid[...]) + dot(hi, t_lo[...]) + dot(lo, t_hi[...])
        return (small + (dot(hi, t_mid[...]) + dot(mid, t_hi[...]))) + dot(hi, t_hi[...])

    f = jnp.concatenate([fir(ext[:, 0:384]), fir(ext[:, 256:640])], axis=1)
    lane = lax.broadcasted_iota(jnp.int32, (1, 512), 1)
    low = jnp.where(chan == 0, TN, 0)
    high = jnp.where(chan == ends, TN + n, 512)
    f = jnp.where((lane >= low) & (lane < high), f, 0.0)
    hi, lo = split2(jnp.abs(f))
    first = dot(hi[:, 0:384], band[...]) + dot(lo[:, 0:384], band[...])
    second = dot(hi[:, 256:512], band[0:256, 0:128]) + dot(lo[:, 256:512], band[0:256, 0:128])
    summed = jnp.concatenate([first, second], axis=1)
    norm = f[:, TN : TN + n] / (summed * (1.0 / (2 * TN + 1)) + EPS)
    for s in range(n // SEG):
        x = norm[:, s * SEG : (s + 1) * SEG]
        p = dot(jnp.concatenate(split2(x), axis=1), fwd[...])
        spec = p[:, :SEG] + p[:, SEG:]
        sq = spec * spec
        amp = jnp.sqrt(sq + pltpu.roll(sq, SEG // 2, 1))
        mean_amp = dot(jnp.concatenate(split2(amp), axis=1), mean[...]) + EPS
        z = spec * (weight[...] / jnp.maximum(amp, FLOOR * mean_amp))
        q = dot(jnp.concatenate(split2(z), axis=1), inv[...])
        out[:, s * SEG : (s + 1) * SEG] = (q[:, :SEG] + q[:, SEG:]).astype(BF)


def front(raw, left, right, toep, weight, rows=256):
    count, n = raw.shape
    fwd, inv, band, mean = (jnp.asarray(t) for t in tables())
    whole = lambda a: pl.BlockSpec(a.shape, lambda i: (0,) * a.ndim)
    blk = lambda w: pl.BlockSpec((rows, w), lambda i: (i, 0))
    return pl.pallas_call(
        front_kernel,
        grid=(count // rows,),
        in_specs=[blk(n), blk(HALO), blk(HALO)] + [whole(a) for a in (toep, weight, fwd, inv, band, mean)],
        out_specs=blk(n),
        out_shape=jax.ShapeDtypeStruct((count, n), BF),
        scratch_shapes=[pltpu.VMEM((rows, 640), F32)] + [pltpu.VMEM((384, 256), BF)] * 3,
        compiler_params=pltpu.CompilerParams(vmem_limit_bytes=40 << 20),
        name="front",
    )(raw, left, right, toep, weight, fwd, inv, band, mean)


def corr_kernel(src, rec, out, lagged):
    count, total = src.shape[0], rec.shape[1]
    blocks = total // 128

    @pl.when(pl.program_id(0) == 0)
    def _():
        @pl.loop(0, count)
        def _(k):
            base = pl.multiple_of(k * LPAD, 16)
            for j in range(-1, blocks):
                row = src[pl.ds(k, 1), pl.ds((j + 1) * 128, 256)]
                rolled = pltpu.roll(jnp.broadcast_to(row, (128, 256)), 0, 1, stride=1, stride_axis=0)
                tile = rolled[:, 128:].astype(BF)
                if j >= 0:
                    lagged[pl.ds(base, 128), j * 128 : (j + 1) * 128] = tile
                if j < blocks - 1:
                    lagged[pl.ds(base + 128, LPAD - 128), (j + 1) * 128 : (j + 2) * 128] = tile[: LPAD - 128]

    scale = total**-0.5

    @pl.loop(0, count)
    def _(k):
        base = pl.multiple_of(k * LPAD, 16)
        acc = lax.dot_general(
            lagged[pl.ds(base, LPAD), :], rec[...], (((1,), (1,)), ((), ())), preferred_element_type=F32
        )
        out[k] = acc[:LAGS] * scale


def corr(src, rec, cols=256):
    total_rec, total = rec.shape
    count = src.shape[0]
    return pl.pallas_call(
        corr_kernel,
        grid=(total_rec // cols,),
        in_specs=[
            pl.BlockSpec(src.shape, lambda i: (0, 0)),
            pl.BlockSpec((cols, total), lambda i: (i, 0)),
        ],
        out_specs=pl.BlockSpec((count, LAGS, cols), lambda i: (0, 0, i)),
        out_shape=jax.ShapeDtypeStruct((count, LAGS, total_rec), F32),
        scratch_shapes=[pltpu.VMEM((count * LPAD, total), BF)],
        compiler_params=pltpu.CompilerParams(vmem_limit_bytes=56 << 20),
        name="corr",
    )(src, rec)


def lag_source(sources):
    total = sources.shape[1]
    left = 256 - HALF
    return jnp.pad(sources, ((0, 0), (left, HALF))).astype(F32)


def toeplitz(fir_taps):
    diff = lax.broadcasted_iota(jnp.int32, (384, 256), 0) - lax.broadcasted_iota(jnp.int32, (384, 256), 1)
    out = jnp.zeros((384, 256), F32)
    for k in range(fir_taps.shape[0]):
        out = jnp.where(diff == k, fir_taps[k], out)
    return out


def shards(raw_data, fir_taps, spectral_weight):
    channels_dev, samples_dev = raw_data.shape
    chan_count = lax.axis_size("chan")
    tm_count = lax.axis_size("tm")
    ends = chan_count - 1
    left = lax.ppermute(raw_data[:, samples_dev - HALO :], "chan", [(i, i + 1) for i in range(ends)])
    right = lax.ppermute(raw_data[:, :HALO], "chan", [(i + 1, i) for i in range(ends)])
    weight = jnp.concatenate([spectral_weight, spectral_weight])[None, :]
    whitened = front(raw_data, left, right, toeplitz(fir_taps), weight)
    source_dev = 128 // chan_count
    stride = channels_dev * tm_count // 128
    own = whitened[::stride]
    every = lax.all_gather(own, "chan", axis=1, tiled=True)
    every = lax.all_gather(every, "tm", axis=0, tiled=True)
    sources = lax.dynamic_slice_in_dim(every, lax.axis_index("chan") * source_dev, source_dev, 0)
    receivers = lax.all_gather(whitened, "chan", axis=1, tiled=True)
    return corr(lag_source(sources), receivers)


def solution(mesh):
    in_specs = (P("tm", "chan"), P(), P())
    out_specs = P("chan", None, "tm")
    return jax.shard_map(shards, mesh=mesh, in_specs=in_specs, out_specs=out_specs, check_vma=False)
```

```python
import jax
import jax.numpy as jnp
import ml_dtypes
import numpy as np
from jax import lax
from jax.experimental import pallas as pl
from jax.experimental.pallas import tpu as pltpu
from jax.sharding import PartitionSpec as P

HK = 16
TN = 64
SEG = 128
HALF = 100
LAGS = 201
EPS = 1e-06
FLOOR = 0.5
HALO = HK + TN
BF = jnp.bfloat16
F32 = jnp.float32


def split_np(table):
    table = np.asarray(table, np.float32)
    hi = table.astype(ml_dtypes.bfloat16)
    lo = (table - hi.astype(np.float32)).astype(ml_dtypes.bfloat16)
    return hi, lo


def tables():
    t, f = np.arange(SEG), np.arange(SEG // 2)
    angle = 2.0 * np.pi * ((t[:, None] * f[None, :]) % SEG) / SEG
    forward = np.concatenate([np.cos(angle), np.sin(angle)], axis=1)
    weight = np.where(f == 0, 1.0, 2.0)[:, None]
    inverse = np.concatenate([np.cos(angle).T * weight, np.sin(angle).T * weight]) / np.sqrt(SEG)
    stacked = []
    for table in (forward, inverse):
        row = np.concatenate(split_np(table), axis=1)
        stacked.append(np.concatenate([row, row], axis=0))
    i, o = np.arange(384)[:, None], np.arange(256)[None, :]
    band = ((i - o >= 0) & (i - o <= 2 * TN)).astype(ml_dtypes.bfloat16)
    mean = np.full((256, 128), 1.0 / 128, ml_dtypes.bfloat16)
    return stacked[0], stacked[1], band, mean


def dot(a, b):
    return jnp.dot(a, b, preferred_element_type=F32)


def split2(x):
    hi = x.astype(BF)
    return hi, (x - hi.astype(F32)).astype(BF)


def split3(x):
    hi = x.astype(BF)
    rest = x - hi.astype(F32)
    mid = rest.astype(BF)
    return hi, mid, (rest - mid.astype(F32)).astype(BF)


def front_kernel(raw, left, right, toep, weight, fwd, inv, band, mean, out, ext, t_hi, t_mid, t_lo):
    chan = lax.axis_index("chan")
    ends = lax.axis_size("chan") - 1

    @pl.when(pl.program_id(0) == 0)
    def _():
        rows = jnp.broadcast_to(toep[...], (256, 384))
        hi, mid, lo = split3(pltpu.roll(rows, 0, 1, stride=1, stride_axis=0).T)
        t_hi[...] = hi
        t_mid[...] = mid
        t_lo[...] = lo

    n = raw.shape[1]
    ext[:, 0:HALO] = left[...]
    ext[:, HALO : HALO + n] = raw[...]
    ext[:, HALO + n : 2 * HALO + n] = right[...]
    ext[:, 2 * HALO + n :] = jnp.zeros((ext.shape[0], ext.shape[1] - 2 * HALO - n), F32)

    def fir(x):
        hi, mid, lo = split3(x)
        small = dot(mid, t_mid[...]) + dot(hi, t_lo[...]) + dot(lo, t_hi[...])
        return (small + (dot(hi, t_mid[...]) + dot(mid, t_hi[...]))) + dot(hi, t_hi[...])

    f = jnp.concatenate([fir(ext[:, 0:384]), fir(ext[:, 256:640])], axis=1)
    lane = lax.broadcasted_iota(jnp.int32, (1, 512), 1)
    low = jnp.where(chan == 0, TN, 0)
    high = jnp.where(chan == ends, TN + n, 512)
    f = jnp.where((lane >= low) & (lane < high), f, 0.0)
    hi, lo = split2(jnp.abs(f))
    first = dot(hi[:, 0:384], band[...]) + dot(lo[:, 0:384], band[...])
    second = dot(hi[:, 256:512], band[0:256, 0:128]) + dot(lo[:, 256:512], band[0:256, 0:128])
    summed = jnp.concatenate([first, second], axis=1)
    norm = f[:, TN : TN + n] / (summed * (1.0 / (2 * TN + 1)) + EPS)
    for s in range(n // SEG):
        x = norm[:, s * SEG : (s + 1) * SEG]
        p = dot(jnp.concatenate(split2(x), axis=1), fwd[...])
        spec = p[:, :SEG] + p[:, SEG:]
        sq = spec * spec
        amp = jnp.sqrt(sq + pltpu.roll(sq, SEG // 2, 1))
        mean_amp = dot(jnp.concatenate(split2(amp), axis=1), mean[...]) + EPS
        z = spec * (weight[...] / jnp.maximum(amp, FLOOR * mean_amp))
        q = dot(jnp.concatenate(split2(z), axis=1), inv[...])
        out[:, s * SEG : (s + 1) * SEG] = (q[:, :SEG] + q[:, SEG:]).astype(BF)


def front(raw, left, right, toep, weight, rows=256):
    count, n = raw.shape
    fwd, inv, band, mean = (jnp.asarray(t) for t in tables())
    whole = lambda a: pl.BlockSpec(a.shape, lambda i: (0,) * a.ndim)
    blk = lambda w: pl.BlockSpec((rows, w), lambda i: (i, 0))
    return pl.pallas_call(
        front_kernel,
        grid=(count // rows,),
        in_specs=[blk(n), blk(HALO), blk(HALO)] + [whole(a) for a in (toep, weight, fwd, inv, band, mean)],
        out_specs=blk(n),
        out_shape=jax.ShapeDtypeStruct((count, n), BF),
        scratch_shapes=[pltpu.VMEM((rows, 640), F32)] + [pltpu.VMEM((384, 256), BF)] * 3,
        compiler_params=pltpu.CompilerParams(vmem_limit_bytes=40 << 20),
        name="front",
    )(raw, left, right, toep, weight, fwd, inv, band, mean)


WIDE = 384
COLS = 256
PIECES = 4


def build_lags(z, lagged, total):
    lane = lax.broadcasted_iota(jnp.int32, (8, 128), 1)
    blocks = total // 128

    @pl.loop(0, 64)
    def _(p):
        shift = p * 2
        tiles = []
        for one in (shift, shift + 1):
            rolled = [pltpu.roll(z[:, j * 128 : (j + 1) * 128], one, 1) for j in range(1, blocks + 3)]
            tiles.append([jnp.where(lane < one, rolled[j], rolled[j + 1]) for j in range(blocks + 1)])
        pairs = [jnp.concatenate([tiles[0][j], tiles[1][j]], axis=0).astype(BF) for j in range(blocks + 1)]

        @pl.when(shift + HALF < LAGS)
        def _():
            row = pl.ds(pl.multiple_of((shift + HALF) * 8, 16), 16)
            for j in range(blocks):
                lagged[row, j * 128 : (j + 1) * 128] = pairs[j]

        @pl.when(shift >= 128 - HALF)
        def _():
            row = pl.ds(pl.multiple_of((shift - (128 - HALF)) * 8, 16), 16)
            for j in range(blocks):
                lagged[row, j * 128 : (j + 1) * 128] = pairs[j + 1]


def corr_kernel(wh, own_src, out, rec, lagged, z, stage, own_sem, send, recv, src_send, src_recv, out_sem):
    tm, me = lax.axis_index("tm"), lax.axis_index("chan")
    n_tm, n_chan = lax.axis_size("tm"), lax.axis_size("chan")
    count, n = wh.shape
    total = n * n_chan
    chunks = count // COLS
    y, x, core = me // 4, (me // 2) % 2, me % 2
    n_y = n_chan // 4
    up, down, far = (y + 1) % n_y, (y + n_y - 1) % n_y, (y + 2) % n_y

    def at(yy, xx, cc):
        return (yy * 2 + xx) * 2 + cc

    to_x, to_u, to_d, to_s = at(y, 1 - x, core), at(up, x, core), at(down, x, core), at(y, x, 1 - core)

    def lanes(b):
        return pl.ds(pl.multiple_of(b * n, 128), n)

    def signal(t, c):
        pl.semaphore_signal(
            pltpu.get_barrier_semaphore(), inc=1, device_id=(t, c), device_id_type=pl.DeviceIdType.MESH
        )

    per = n_chan // n_tm
    targets = [(t, per * tm + h) for t in range(n_tm) for h in range(per)]
    origins = [(me // per, c) for c in range(n_chan)]
    for t, c in targets + origins:

        @pl.when((t != tm) | (c != me))
        def _():
            signal(t, c)

    for c in (to_x, to_u, to_d, to_s):
        signal(tm, c)
    barrier = pltpu.get_barrier_semaphore()
    mine = me // per == tm

    @pl.when(mine)
    def _():
        pl.semaphore_wait(barrier, len(targets) + len(origins) + 2)

    @pl.when(jnp.logical_not(mine))
    def _():
        pl.semaphore_wait(barrier, len(targets) + len(origins) + 4)

    def src_copy(t, c, h, send_slot, who):
        return pltpu.make_async_remote_copy(
            src_ref=own_src.at[h * 8 : (h + 1) * 8, :],
            dst_ref=z.at[:, pl.ds(pl.multiple_of(256 + who * n, 128), n)],
            send_sem=src_send.at[send_slot],
            recv_sem=src_recv.at[who],
            device_id=(t, c),
            device_id_type=pl.DeviceIdType.MESH,
        )

    for slot, (t, c) in enumerate(targets):

        @pl.when((t != tm) | (c != me))
        def _():
            src_copy(t, c, slot % per, slot, me).start()

    def copy(s_kind, r_kind, c, target, block, half=None, source=None):
        size = COLS if half is None else COLS // 2
        start = c * COLS + (0 if half is None else half * size)
        rows = pl.ds(pl.multiple_of(start, 128), size)
        return pltpu.make_async_remote_copy(
            src_ref=rec.at[rows, lanes(block)] if source is None else source.at[rows, :],
            dst_ref=rec.at[rows, lanes(block)],
            send_sem=send.at[s_kind, c],
            recv_sem=recv.at[r_kind, c],
            device_id=(tm, target),
            device_id_type=pl.DeviceIdType.MESH,
        )

    blk_p, blk_u, blk_d = at(y, 1 - x, core), at(up, x, core), at(down, x, core)
    blk_up, blk_dp = at(up, 1 - x, core), at(down, 1 - x, core)
    blk_f, blk_fp = at(far, x, core), at(far, 1 - x, core)

    def sends(c, name):
        table = {
            "own": [
                (0, 0, c, to_x, me, None, wh),
                (1, 2, c, to_u, me, None, wh),
                (2, 1, c, to_d, me, None, wh),
                (3, 8, c, to_s, me, None, wh),
            ],
            "p": [(4, 4, c, to_u, blk_p), (5, 3, c, to_d, blk_p), (6, 9, c, to_s, blk_p)],
            "u": [(7, 6, c, to_d, blk_u, 1), (8, 10, c, to_s, blk_u)],
            "d": [(9, 5, c, to_u, blk_d, 0), (10, 11, c, to_s, blk_d)],
            "f": [(11, 7, c, to_x, blk_f), (12, 14, c, to_s, blk_f)],
            "up": [(13, 12, c, to_s, blk_up)],
            "dp": [(14, 13, c, to_s, blk_dp)],
            "fp": [(15, 15, c, to_s, blk_fp)],
        }
        return [copy(*one) for one in table[name]]

    def start(c, *names):
        for name in names:
            for one in sends(c, name):
                one.start()

    def arrived(c, r_kind, block, half=None):
        copy(0, r_kind, c, to_x, block, half=half).wait_recv()

    own_copy = pltpu.make_async_copy(wh, rec.at[:, lanes(me)], own_sem)
    start(0, "own")
    own_copy.start()
    z[:, 0:256] = jnp.zeros((8, 256), F32)
    z[:, 256 + total :] = jnp.zeros((8, 128), F32)

    @pl.when(mine)
    def _():
        z[:, pl.ds(pl.multiple_of(256 + me * n, 128), n)] = own_src[pl.ds(pl.multiple_of((me % per) * 8, 8), 8), :]

    start(1, "own")
    own_copy.wait()
    for c in range(n_chan):

        @pl.when((me // per != tm) | (c != me))
        def _():
            src_copy(tm, to_x, 0, 0, c).wait_recv()

    build_lags(z, lagged, total)
    scale = total**-0.5
    used = LAGS * 8
    step = -(-used // PIECES // 16) * 16

    def out_copy(c):
        return pltpu.make_async_copy(
            stage.at[c % 2], out.at[:, :, pl.ds(pl.multiple_of(c * COLS, 128), COLS)], out_sem.at[c % 2]
        )

    def piece(c, i):
        first = i * step
        rows = min(step, used - first)
        full = -(-rows // 16) * 16
        acc = lax.dot_general(
            lagged[first : first + full, :],
            rec[pl.ds(pl.multiple_of(c * COLS, 128), COLS), :],
            (((1,), (1,)), ((), ())),
            preferred_element_type=F32,
        )
        stage[c % 2, first // 8 : (first + rows) // 8] = (acc[:rows] * scale).reshape(rows // 8, 8, COLS)

    @pl.loop(0, chunks + 1)
    def _(c):
        live, ready = c < chunks, c >= 1
        b = c - 1

        @pl.when(live & (c >= 1) & (c + 1 < chunks))
        def _():
            start(c + 1, "own")

        @pl.when(live)
        def _():
            arrived(c, 0, blk_p)
            start(c, "p")

        @pl.when(ready)
        def _():
            for kind, yy in ((8, y), (9, y), (10, up), (11, down), (12, up), (13, down), (14, far), (15, far)):
                xx = x if kind in (8, 10, 11, 14) else 1 - x
                arrived(b, kind, at(yy, xx, 1 - core))

            @pl.when(b >= 2)
            def _():
                out_copy(b - 2).wait()

            piece(b, 0)

        @pl.when(live)
        def _():
            arrived(c, 1, blk_u)
            start(c, "u")
            arrived(c, 2, blk_d)
            start(c, "d")

        @pl.when(ready)
        def _():
            piece(b, 1)

        @pl.when(live)
        def _():
            arrived(c, 5, blk_f, half=0)
            arrived(c, 6, blk_f, half=1)
            start(c, "f")

        @pl.when(ready)
        def _():
            piece(b, 2)

        @pl.when(live)
        def _():
            arrived(c, 3, blk_up)
            start(c, "up")
            arrived(c, 4, blk_dp)
            start(c, "dp")

        @pl.when(ready)
        def _():
            piece(b, 3)
            out_copy(b).start()

        @pl.when(live)
        def _():
            arrived(c, 7, blk_fp)
            start(c, "fp")

    @pl.loop(0, chunks)
    def _(c):
        for name in ("own", "p", "u", "d", "f", "up", "dp", "fp"):
            for one in sends(c, name):
                one.wait_send()

    for slot, (t, c) in enumerate(targets):

        @pl.when((t != tm) | (c != me))
        def _():
            src_copy(t, c, slot % per, slot, me).wait_send()

    out_copy(chunks - 2).wait()
    out_copy(chunks - 1).wait()


def corr(wh, own_src, n_tm, n_chan):
    count, n = wh.shape
    total = n * n_chan
    chunks = count // COLS
    dma = pltpu.SemaphoreType.DMA
    flops = 2 * LAGS * 8 * count * total
    return pl.pallas_call(
        corr_kernel,
        in_specs=[pl.BlockSpec(memory_space=pl.ANY), pl.BlockSpec(memory_space=pltpu.VMEM)],
        out_specs=pl.BlockSpec(memory_space=pl.ANY),
        out_shape=jax.ShapeDtypeStruct((LAGS, 8, count), F32),
        scratch_shapes=[
            pltpu.VMEM((count, total), BF),
            pltpu.VMEM(((LAGS + 1) * 8, total), BF),
            pltpu.VMEM((8, total + 384), F32),
            pltpu.VMEM((2, LAGS, 8, COLS), F32),
            dma(()),
            dma((16, chunks)),
            dma((16, chunks)),
            dma((16,)),
            dma((n_chan,)),
            dma((2,)),
        ],
        compiler_params=pltpu.CompilerParams(
            collective_id=0, has_side_effects=True, vmem_limit_bytes=58 << 20
        ),
        cost_estimate=pl.CostEstimate(flops=flops, bytes_accessed=3 * count * total, transcendentals=0),
        name="corr",
    )(wh, own_src)


def shards(raw_data, fir_taps, spectral_weight):
    channels_dev, samples_dev = raw_data.shape
    chan_count = lax.axis_size("chan")
    tm_count = lax.axis_size("tm")
    ends = chan_count - 1
    left = lax.ppermute(raw_data[:, samples_dev - HALO :], "chan", [(i, i + 1) for i in range(ends)])
    right = lax.ppermute(raw_data[:, :HALO], "chan", [(i + 1, i) for i in range(ends)])
    taps = jnp.pad(fir_taps, (0, 384 - fir_taps.shape[0]))[None, :]
    weight = jnp.concatenate([spectral_weight, spectral_weight])[None, :]
    whitened = front(raw_data, left, right, taps, weight)
    stride = channels_dev * tm_count // 128
    own = whitened[::stride].astype(F32)
    result = corr(whitened, own, tm_count, chan_count)
    return result.transpose(1, 0, 2)


def solution(mesh):
    in_specs = (P("tm", "chan"), P(), P())
    out_specs = P("chan", None, "tm")
    return jax.shard_map(shards, mesh=mesh, in_specs=in_specs, out_specs=out_specs, check_vma=False)
```

```python
import jax
import jax.numpy as jnp
import ml_dtypes
import numpy as np
from jax import lax
from jax.experimental import pallas as pl
from jax.experimental.pallas import tpu as pltpu
from jax.sharding import PartitionSpec as P

HK = 16
TN = 64
SEG = 128
HALF = 100
LAGS = 201
EPS = 1e-06
FLOOR = 0.5
HALO = HK + TN
BF = jnp.bfloat16
F32 = jnp.float32


def split_np(table):
    table = np.asarray(table, np.float32)
    hi = table.astype(ml_dtypes.bfloat16)
    lo = (table - hi.astype(np.float32)).astype(ml_dtypes.bfloat16)
    return hi, lo


def tables():
    t, f = np.arange(SEG), np.arange(SEG // 2)
    angle = 2.0 * np.pi * ((t[:, None] * f[None, :]) % SEG) / SEG
    forward = np.concatenate([np.cos(angle), np.sin(angle)], axis=1)
    weight = np.where(f == 0, 1.0, 2.0)[:, None]
    inverse = np.concatenate([np.cos(angle).T * weight, np.sin(angle).T * weight]) / np.sqrt(SEG)
    stacked = []
    for table in (forward, inverse):
        row = np.concatenate(split_np(table), axis=1)
        stacked.append(np.concatenate([row, row], axis=0))
    i, o = np.arange(384)[:, None], np.arange(256)[None, :]
    band = ((i - o >= 0) & (i - o <= 2 * TN)).astype(ml_dtypes.bfloat16)
    mean = np.full((256, 128), 1.0 / 128, ml_dtypes.bfloat16)
    return stacked[0], stacked[1], band, mean


def dot(a, b):
    return jnp.dot(a, b, preferred_element_type=F32)


def split2(x):
    hi = x.astype(BF)
    return hi, (x - hi.astype(F32)).astype(BF)


def split3(x):
    hi = x.astype(BF)
    rest = x - hi.astype(F32)
    mid = rest.astype(BF)
    return hi, mid, (rest - mid.astype(F32)).astype(BF)


def whiten_rows(left, raw, right, ext, taps, weight, fwd, inv, band, mean):
    rows, n = raw.shape
    here = pl.ds(0, rows)
    chan, ends = lax.axis_index("chan"), lax.axis_size("chan") - 1
    ext[here, 0:HALO] = left[:, left.shape[1] - HALO :]
    ext[here, HALO : HALO + n] = raw
    ext[here, HALO + n : 2 * HALO + n] = right[:, :HALO]
    t_hi, t_mid, t_lo = taps

    def fir(x):
        hi, mid, lo = split3(x)
        small = dot(mid, t_mid[...]) + dot(hi, t_lo[...]) + dot(lo, t_hi[...])
        return (small + (dot(hi, t_mid[...]) + dot(mid, t_hi[...]))) + dot(hi, t_hi[...])

    f = jnp.concatenate([fir(ext[here, 0:384]), fir(ext[here, 256:640])], axis=1)
    lane = lax.broadcasted_iota(jnp.int32, (1, 512), 1)
    low = jnp.where(chan == 0, TN, 0)
    high = jnp.where(chan == ends, TN + n, 512)
    f = jnp.where((lane >= low) & (lane < high), f, 0.0)
    hi, lo = split2(jnp.abs(f))
    first = dot(hi[:, 0:384], band[...]) + dot(lo[:, 0:384], band[...])
    second = dot(hi[:, 256:512], band[0:256, 0:128]) + dot(lo[:, 256:512], band[0:256, 0:128])
    summed = jnp.concatenate([first, second], axis=1)
    norm = f[:, TN : TN + n] / (summed * (1.0 / (2 * TN + 1)) + EPS)
    parts = []
    for s in range(n // SEG):
        x = norm[:, s * SEG : (s + 1) * SEG]
        p = dot(jnp.concatenate(split2(x), axis=1), fwd[...])
        spec = p[:, :SEG] + p[:, SEG:]
        sq = spec * spec
        amp = jnp.sqrt(sq + pltpu.roll(sq, SEG // 2, 1))
        mean_amp = dot(jnp.concatenate(split2(amp), axis=1), mean[...]) + EPS
        z = spec * (weight[...] / jnp.maximum(amp, FLOOR * mean_amp))
        q = dot(jnp.concatenate(split2(z), axis=1), inv[...])
        parts.append((q[:, :SEG] + q[:, SEG:]).astype(BF))
    return jnp.concatenate(parts, axis=1)


AHEAD = 4
HALOS_AHEAD = 7
LANES = 128
COLS = 256
ROWS = 128
PIECES = 4


def build_lags(z, lagged, total, part, parts):
    lane = lax.broadcasted_iota(jnp.int32, (8, 128), 1)
    blocks = total // 128

    @pl.loop(part * (64 // parts), (part + 1) * (64 // parts))
    def _(p):
        shift = p * 2
        tiles = []
        for one in (shift, shift + 1):
            rolled = [pltpu.roll(z[:, j * 128 : (j + 1) * 128], one, 1) for j in range(1, blocks + 3)]
            tiles.append([jnp.where(lane < one, rolled[j], rolled[j + 1]) for j in range(blocks + 1)])
        pairs = [jnp.concatenate([tiles[0][j], tiles[1][j]], axis=0).astype(BF) for j in range(blocks + 1)]

        @pl.when(shift + HALF < LAGS)
        def _():
            row = pl.ds(pl.multiple_of((shift + HALF) * 8, 16), 16)
            for j in range(blocks):
                lagged[row, j * 128 : (j + 1) * 128] = pairs[j]

        @pl.when(shift >= 128 - HALF)
        def _():
            row = pl.ds(pl.multiple_of((shift - (128 - HALF)) * 8, 16), 16)
            for j in range(blocks):
                lagged[row, j * 128 : (j + 1) * 128] = pairs[j + 1]


def corr_kernel(
    raw_hbm, taps, weight, fwd, inv, band, mean, out,
    rec, lagged, z, stage, raw, wh, own_src, ext, left, right, few, few_left, few_right, t_hi, t_mid, t_lo,
    raw_sem, own_sem, send, recv, src_send, src_recv, out_sem, halo_send, halo_recv,
):
    tm, me = lax.axis_index("tm"), lax.axis_index("chan")
    n_tm, n_chan = lax.axis_size("tm"), lax.axis_size("chan")
    count, n = wh.shape
    total = n * n_chan
    chunks, steps = count // COLS, count // ROWS
    y, x, core = me // 4, (me // 2) % 2, me % 2
    n_y = n_chan // 4
    up, down, far = (y + 1) % n_y, (y + n_y - 1) % n_y, (y + 2) % n_y

    def at(yy, xx, cc):
        return (yy * 2 + xx) * 2 + cc

    raw_copy = pltpu.make_async_copy(raw_hbm, raw, raw_sem)
    raw_copy.start()
    to_x, to_u, to_d, to_s = at(y, 1 - x, core), at(up, x, core), at(down, x, core), at(y, x, 1 - core)

    def lanes(b):
        return pl.ds(pl.multiple_of(b * n, 128), n)

    def signal(t, c):
        pl.semaphore_signal(
            pltpu.get_barrier_semaphore(), inc=1, device_id=(t, c), device_id_type=pl.DeviceIdType.MESH
        )

    per = n_chan // n_tm
    targets = [(t, per * tm + h) for t in range(n_tm) for h in range(per)]
    origins = [(me // per, c) for c in range(n_chan)]
    for t, c in targets + origins:

        @pl.when((t != tm) | (c != me))
        def _():
            signal(t, c)

    before, after = (me + n_chan - 1) % n_chan, (me + 1) % n_chan
    for c in (to_x, to_u, to_d, to_s, before, after):
        signal(tm, c)
    barrier = pltpu.get_barrier_semaphore()
    mine = me // per == tm

    @pl.when(mine)
    def _():
        pl.semaphore_wait(barrier, len(targets) + len(origins) + 4)

    @pl.when(jnp.logical_not(mine))
    def _():
        pl.semaphore_wait(barrier, len(targets) + len(origins) + 6)

    def src_copy(t, c, h, send_slot, who):
        return pltpu.make_async_remote_copy(
            src_ref=own_src.at[h * 8 : (h + 1) * 8, :],
            dst_ref=z.at[:, pl.ds(pl.multiple_of(256 + who * n, 128), n)],
            send_sem=src_send.at[send_slot],
            recv_sem=src_recv.at[who],
            device_id=(t, c),
            device_id_type=pl.DeviceIdType.MESH,
        )

    def copy(s_kind, r_kind, c, target, block, half=None, source=None):
        size = ROWS if half is None else ROWS // 2
        start = c * ROWS + (0 if half is None else half * size)
        rows = pl.ds(pl.multiple_of(start, ROWS // 2), size)
        return pltpu.make_async_remote_copy(
            src_ref=rec.at[rows, lanes(block)] if source is None else source.at[rows, :],
            dst_ref=rec.at[rows, lanes(block)],
            send_sem=send.at[s_kind, c],
            recv_sem=recv.at[r_kind, c],
            device_id=(tm, target),
            device_id_type=pl.DeviceIdType.MESH,
        )

    blk_p, blk_u, blk_d = at(y, 1 - x, core), at(up, x, core), at(down, x, core)
    blk_up, blk_dp = at(up, 1 - x, core), at(down, 1 - x, core)
    blk_f, blk_fp = at(far, x, core), at(far, 1 - x, core)

    def sends(c, name):
        table = {
            "own": [
                (0, 0, c, to_x, me, None, wh),
                (1, 2, c, to_u, me, None, wh),
                (2, 1, c, to_d, me, None, wh),
                (3, 8, c, to_s, me, None, wh),
            ],
            "p": [(4, 4, c, to_u, blk_p), (5, 3, c, to_d, blk_p), (6, 9, c, to_s, blk_p)],
            "u": [(7, 6, c, to_d, blk_u, 1), (8, 10, c, to_s, blk_u)],
            "d": [(9, 5, c, to_u, blk_d, 0), (10, 11, c, to_s, blk_d)],
            "f": [(11, 7, c, to_x, blk_f), (12, 14, c, to_s, blk_f)],
            "up": [(13, 12, c, to_s, blk_up)],
            "dp": [(14, 13, c, to_s, blk_dp)],
            "fp": [(15, 15, c, to_s, blk_fp)],
        }
        return [copy(*one) for one in table[name]]

    def start(c, *names):
        for name in names:
            for one in sends(c, name):
                one.start()

    def arrived(c, r_kind, block, half=None):
        copy(0, r_kind, c, to_x, block, half=half).wait_recv()

    tables = ((t_hi, t_mid, t_lo), weight, fwd, inv, band, mean)
    has_left, has_right = me > 0, me < n_chan - 1
    last_lanes, first_lanes = pl.ds(n - LANES, LANES), pl.ds(0, LANES)

    def halo_to_right(source, target, c):
        return pltpu.make_async_remote_copy(
            src_ref=source, dst_ref=target, send_sem=halo_send.at[0, c], recv_sem=halo_recv.at[0, c],
            device_id=(tm, after), device_id_type=pl.DeviceIdType.MESH,
        )

    def halo_to_left(source, target, c):
        return pltpu.make_async_remote_copy(
            src_ref=source, dst_ref=target, send_sem=halo_send.at[1, c], recv_sem=halo_recv.at[1, c],
            device_id=(tm, before), device_id_type=pl.DeviceIdType.MESH,
        )

    def step_rows(c):
        return pl.ds(pl.multiple_of(c * ROWS, ROWS), ROWS)

    def halo_pair(c):
        rows = step_rows(c)
        return (
            halo_to_right(raw.at[rows, last_lanes], left.at[rows, :], c),
            halo_to_left(raw.at[rows, first_lanes], right.at[rows, :], c),
        )

    few_pair = (
        halo_to_right(few.at[:, last_lanes], few_left, steps),
        halo_to_left(few.at[:, first_lanes], few_right, steps),
    )

    def on_sides(pair, name, flip=False):
        sides = (has_left, has_right) if flip else (has_right, has_left)
        for one, there in zip(pair, sides):
            pl.when(there)(getattr(one, name))

    def own_copy(c):
        return pltpu.make_async_copy(wh.at[step_rows(c), :], rec.at[step_rows(c), lanes(me)], own_sem.at[c])

    def whiten_step(c):
        rows = step_rows(c)
        on_sides(halo_pair(c), "wait_recv", flip=True)
        wh[rows, :] = whiten_rows(left[rows, :], raw[rows, :], right[rows, :], ext, *tables)
        start(c, "own")
        own_copy(c).start()

    raw_copy.wait()
    stride = count * n_tm // (8 * n_chan)
    for k in range(8 * per):
        few[k : k + 1, :] = raw[k * stride : k * stride + 1, :]
    on_sides(few_pair, "start")
    for c in range(min(HALOS_AHEAD, steps)):
        on_sides(halo_pair(c), "start")

    @pl.when(me == 0)
    def _():
        left[...] = jnp.zeros(left.shape, F32)
        few_left[...] = jnp.zeros(few_left.shape, F32)

    @pl.when(me == n_chan - 1)
    def _():
        right[...] = jnp.zeros(right.shape, F32)
        few_right[...] = jnp.zeros(few_right.shape, F32)

    rolled = pltpu.roll(jnp.broadcast_to(taps[...], (256, 384)), 0, 1, stride=1, stride_axis=0)
    hi, mid, lo = split3(rolled.T)
    t_hi[...] = hi
    t_mid[...] = mid
    t_lo[...] = lo
    ext[...] = jnp.zeros(ext.shape, F32)
    z[:, 0:256] = jnp.zeros((8, 256), F32)
    z[:, 256 + total :] = jnp.zeros((8, 128), F32)
    on_sides(few_pair, "wait_recv", flip=True)
    own_src[...] = whiten_rows(few_left[...], few[...], few_right[...], ext, *tables).astype(F32)

    for slot, (t, c) in enumerate(targets):

        @pl.when((t != tm) | (c != me))
        def _():
            src_copy(t, c, slot % per, slot, me).start()

    @pl.when(mine)
    def _():
        z[:, pl.ds(pl.multiple_of(256 + me * n, 128), n)] = own_src[pl.ds(pl.multiple_of((me % per) * 8, 8), 8), :]

    @pl.loop(0, min(AHEAD, steps))
    def _(c):
        whiten_step(c)

    def lag_part(part, parts):
        @pl.when(part == 0)
        def _():
            for c in range(n_chan):

                @pl.when((me // per != tm) | (c != me))
                def _():
                    src_copy(tm, to_x, 0, 0, c).wait_recv()

        build_lags(z, lagged, total, part, parts)

    scale = total**-0.5
    used = LAGS * 8
    step = -(-used // PIECES // 16) * 16

    def out_copy(c):
        return pltpu.make_async_copy(
            stage.at[c % 2], out.at[:, :, pl.ds(pl.multiple_of(c * COLS, 128), COLS)], out_sem.at[c % 2]
        )

    def piece(c, i):
        first = i * step
        rows = min(step, used - first)
        full = -(-rows // 16) * 16
        acc = lax.dot_general(
            lagged[first : first + full, :],
            rec[pl.ds(pl.multiple_of(c * COLS, 128), COLS), :],
            (((1,), (1,)), ((), ())),
            preferred_element_type=F32,
        )
        stage[c % 2, first // 8 : (first + rows) // 8] = (acc[:rows] * scale).reshape(rows // 8, 8, COLS)

    def near(c):
        @pl.when(c < steps)
        def _():
            @pl.when(c + HALOS_AHEAD < steps)
            def _():
                on_sides(halo_pair(c + HALOS_AHEAD), "start")

            @pl.when(c + AHEAD < steps)
            def _():
                whiten_step(c + AHEAD)

            arrived(c, 0, blk_p)
            start(c, "p")

    def ring(c):
        @pl.when(c < steps)
        def _():
            arrived(c, 1, blk_u)
            start(c, "u")
            arrived(c, 2, blk_d)
            start(c, "d")

        @pl.when((c >= 1) & (c <= steps))
        def _():
            arrived(c - 1, 5, blk_f, half=0)
            arrived(c - 1, 6, blk_f, half=1)
            start(c - 1, "f")

    def last(c):
        @pl.when((c >= 1) & (c <= steps))
        def _():
            arrived(c - 1, 3, blk_up)
            start(c - 1, "up")
            arrived(c - 1, 4, blk_dp)
            start(c - 1, "dp")

        @pl.when((c >= 2) & (c <= steps + 1))
        def _():
            arrived(c - 2, 7, blk_fp)
            start(c - 2, "fp")

    def twin(c):
        for kind, yy in ((8, y), (9, y), (10, up), (11, down), (12, up), (13, down), (14, far), (15, far)):
            xx = x if kind in (8, 10, 11, 14) else 1 - x
            arrived(c, kind, at(yy, xx, 1 - core))

    @pl.loop(0, chunks + 2)
    def _(m):
        b = m - 2
        ready = b >= 0

        near(2 * m)

        @pl.when(m < 2)
        def _():
            lag_part(2 * m, 4)

        @pl.when(ready)
        def _():
            for c in (2 * b, 2 * b + 1):
                twin(c)
                own_copy(c).wait()

            @pl.when(b >= 2)
            def _():
                out_copy(b - 2).wait()

            piece(b, 0)

        ring(2 * m)

        @pl.when(ready)
        def _():
            piece(b, 1)

        last(2 * m)
        near(2 * m + 1)

        @pl.when(m < 2)
        def _():
            lag_part(2 * m + 1, 4)

        @pl.when(ready)
        def _():
            piece(b, 2)

        ring(2 * m + 1)

        @pl.when(ready)
        def _():
            piece(b, 3)
            out_copy(b).start()

        last(2 * m + 1)

    @pl.loop(0, steps)
    def _(c):
        for name in ("own", "p", "u", "d", "f", "up", "dp", "fp"):
            for one in sends(c, name):
                one.wait_send()

        on_sides(halo_pair(c), "wait_send")

    on_sides(few_pair, "wait_send")
    for slot, (t, c) in enumerate(targets):

        @pl.when((t != tm) | (c != me))
        def _():
            src_copy(t, c, slot % per, slot, me).wait_send()

    out_copy(chunks - 2).wait()
    out_copy(chunks - 1).wait()


def shards(raw_data, fir_taps, spectral_weight):
    count, n = raw_data.shape
    n_tm, n_chan = lax.axis_size("tm"), lax.axis_size("chan")
    total = n * n_chan
    steps = count // ROWS
    few = 8 * n_chan // n_tm
    taps = jnp.pad(fir_taps, (0, 384 - fir_taps.shape[0]))[None, :]
    weight = jnp.concatenate([spectral_weight, spectral_weight])[None, :]
    consts = [jnp.asarray(t) for t in tables()]
    dma = pltpu.SemaphoreType.DMA
    vmem = pl.BlockSpec(memory_space=pltpu.VMEM)
    hbm = pl.BlockSpec(memory_space=pl.ANY)
    result = pl.pallas_call(
        corr_kernel,
        in_specs=[hbm] + [vmem] * 6,
        out_specs=hbm,
        out_shape=jax.ShapeDtypeStruct((LAGS, 8, count), F32),
        scratch_shapes=[
            pltpu.VMEM((count, total), BF),
            pltpu.VMEM(((LAGS + 1) * 8, total), BF),
            pltpu.VMEM((8, total + 384), F32),
            pltpu.VMEM((2, LAGS, 8, COLS), F32),
            pltpu.VMEM((count, n), F32),
            pltpu.VMEM((count, n), BF),
            pltpu.VMEM((few, n), F32),
            pltpu.VMEM((ROWS, 640), F32),
            pltpu.VMEM((count, LANES), F32),
            pltpu.VMEM((count, LANES), F32),
            pltpu.VMEM((few, n), F32),
            pltpu.VMEM((few, LANES), F32),
            pltpu.VMEM((few, LANES), F32),
            pltpu.VMEM((384, 256), BF),
            pltpu.VMEM((384, 256), BF),
            pltpu.VMEM((384, 256), BF),
            dma(()),
            dma((steps,)),
            dma((16, steps)),
            dma((16, steps)),
            dma((n_tm * (n_chan // n_tm),)),
            dma((n_chan,)),
            dma((2,)),
            dma((2, steps + 1)),
            dma((2, steps + 1)),
        ],
        compiler_params=pltpu.CompilerParams(
            collective_id=0, has_side_effects=True, vmem_limit_bytes=60 << 20
        ),
        name="corr",
    )(raw_data, taps, weight, *consts)
    return result.transpose(1, 0, 2)


def solution(mesh):
    in_specs = (P("tm", "chan"), P(), P())
    out_specs = P("chan", None, "tm")
    return jax.shard_map(shards, mesh=mesh, in_specs=in_specs, out_specs=out_specs, check_vma=False)
```

```python
import jax
import jax.numpy as jnp
import ml_dtypes
import numpy as np
from jax import lax
from jax.experimental import pallas as pl
from jax.experimental.pallas import tpu as pltpu
from jax.sharding import PartitionSpec as P

HK = 16
TN = 64
SEG = 128
HALF = 100
LAGS = 201
EPS = 1e-06
FLOOR = 0.5
HALO = HK + TN
BF = jnp.bfloat16
F32 = jnp.float32


def split_np(table):
    table = np.asarray(table, np.float32)
    hi = table.astype(ml_dtypes.bfloat16)
    lo = (table - hi.astype(np.float32)).astype(ml_dtypes.bfloat16)
    return hi, lo


def tables():
    t, f = np.arange(SEG), np.arange(SEG // 2)
    angle = 2.0 * np.pi * ((t[:, None] * f[None, :]) % SEG) / SEG
    forward = np.concatenate([np.cos(angle), np.sin(angle)], axis=1)
    weight = np.where(f == 0, 1.0, 2.0)[:, None]
    inverse = np.concatenate([np.cos(angle).T * weight, np.sin(angle).T * weight]) / np.sqrt(SEG)
    stacked = []
    for table in (forward, inverse):
        row = np.concatenate(split_np(table), axis=1)
        stacked.append(np.concatenate([row, row], axis=0))
    i, o = np.arange(384)[:, None], np.arange(256)[None, :]
    band = ((i - o >= 0) & (i - o <= 2 * TN)).astype(ml_dtypes.bfloat16)
    return stacked[0], stacked[1], band


def dot(a, b):
    return jnp.dot(a, b, preferred_element_type=F32)


def split2(x):
    hi = x.astype(BF)
    return hi, (x - hi.astype(F32)).astype(BF)


def split3(x):
    hi = x.astype(BF)
    rest = x - hi.astype(F32)
    mid = rest.astype(BF)
    return hi, mid, (rest - mid.astype(F32)).astype(BF)


def whiten_rows(left, raw, right, ext, taps, weight, fwd, inv, band, mean):
    rows, n = raw.shape
    here = pl.ds(0, rows)
    chan, ends = lax.axis_index("chan"), lax.axis_size("chan") - 1
    ext[here, 0:HALO] = left[:, left.shape[1] - HALO :]
    ext[here, HALO : HALO + n] = raw
    ext[here, HALO + n : 2 * HALO + n] = right[:, :HALO]
    t_hi, t_mid, t_lo = taps

    def fir(x):
        hi, mid, lo = split3(x)
        small = dot(mid, t_mid[...]) + dot(hi, t_lo[...]) + dot(lo, t_hi[...])
        return (small + (dot(hi, t_mid[...]) + dot(mid, t_hi[...]))) + dot(hi, t_hi[...])

    f = jnp.concatenate([fir(ext[here, 0:384]), fir(ext[here, 256:640])], axis=1)
    lane = lax.broadcasted_iota(jnp.int32, (1, 512), 1)
    low = jnp.where(chan == 0, TN, 0)
    high = jnp.where(chan == ends, TN + n, 512)
    f = jnp.where((lane >= low) & (lane < high), f, 0.0)
    hi, lo = split2(jnp.abs(f))
    first = dot(hi[:, 0:384], band[...]) + dot(lo[:, 0:384], band[...])
    second = dot(hi[:, 256:512], band[0:256, 0:128]) + dot(lo[:, 256:512], band[0:256, 0:128])
    summed = jnp.concatenate([first, second], axis=1)
    norm = f[:, TN : TN + n] / (summed * (1.0 / (2 * TN + 1)) + EPS)
    parts = []
    for s in range(n // SEG):
        x = norm[:, s * SEG : (s + 1) * SEG]
        p = dot(jnp.concatenate(split2(x), axis=1), fwd[...])
        spec = p[:, :SEG] + p[:, SEG:]
        sq = spec * spec
        amp = jnp.sqrt(sq + pltpu.roll(sq, SEG // 2, 1))
        mean_amp = dot(jnp.concatenate(split2(amp), axis=1), mean[...]) + EPS
        z = spec * (weight[...] / jnp.maximum(amp, FLOOR * mean_amp))
        q = dot(jnp.concatenate(split2(z), axis=1), inv[...])
        parts.append((q[:, :SEG] + q[:, SEG:]).astype(BF))
    return jnp.concatenate(parts, axis=1)


AHEAD = 4
HALOS_AHEAD = 7
LANES = 128
COLS = 256
ROWS = 128
PIECES = 4


def build_lags(z, lagged, total, part, parts):
    lane = lax.broadcasted_iota(jnp.int32, (8, 128), 1)
    blocks = total // 128

    @pl.loop(part * (64 // parts), (part + 1) * (64 // parts))
    def _(p):
        shift = p * 2
        tiles = []
        for one in (shift, shift + 1):
            rolled = [pltpu.roll(z[:, j * 128 : (j + 1) * 128], one, 1) for j in range(1, blocks + 3)]
            tiles.append([jnp.where(lane < one, rolled[j], rolled[j + 1]) for j in range(blocks + 1)])
        pairs = [jnp.concatenate([tiles[0][j], tiles[1][j]], axis=0).astype(BF) for j in range(blocks + 1)]

        @pl.when(shift + HALF < LAGS)
        def _():
            row = pl.ds(pl.multiple_of((shift + HALF) * 8, 16), 16)
            for j in range(blocks):
                lagged[row, j * 128 : (j + 1) * 128] = pairs[j]

        @pl.when(shift >= 128 - HALF)
        def _():
            row = pl.ds(pl.multiple_of((shift - (128 - HALF)) * 8, 16), 16)
            for j in range(blocks):
                lagged[row, j * 128 : (j + 1) * 128] = pairs[j + 1]


def corr_kernel(
    raw_hbm, taps, spectral, fwd, inv, band, out,
    rec, lagged, z, stage, raw, wh, own_src, ext, left, right, few, few_left, few_right, t_hi, t_mid, t_lo, weight, mean,
    raw_sem, own_sem, send, recv, src_send, src_recv, out_sem, halo_send, halo_recv,
):
    tm, me = lax.axis_index("tm"), lax.axis_index("chan")
    n_tm, n_chan = lax.axis_size("tm"), lax.axis_size("chan")
    count, n = wh.shape
    total = n * n_chan
    chunks, steps = count // COLS, count // ROWS
    y, x, core = me // 4, (me // 2) % 2, me % 2
    n_y = n_chan // 4
    up, down, far = (y + 1) % n_y, (y + n_y - 1) % n_y, (y + 2) % n_y

    def at(yy, xx, cc):
        return (yy * 2 + xx) * 2 + cc

    raw_copy = pltpu.make_async_copy(raw_hbm, raw, raw_sem)
    raw_copy.start()
    to_x, to_u, to_d, to_s = at(y, 1 - x, core), at(up, x, core), at(down, x, core), at(y, x, 1 - core)

    def lanes(b):
        return pl.ds(pl.multiple_of(b * n, 128), n)

    def signal(t, c):
        pl.semaphore_signal(
            pltpu.get_barrier_semaphore(), inc=1, device_id=(t, c), device_id_type=pl.DeviceIdType.MESH
        )

    per = n_chan // n_tm
    targets = [(t, per * tm + h) for t in range(n_tm) for h in range(per)]
    origins = [(me // per, c) for c in range(n_chan)]
    for t, c in targets + origins:

        @pl.when((t != tm) | (c != me))
        def _():
            signal(t, c)

    before, after = (me + n_chan - 1) % n_chan, (me + 1) % n_chan
    for c in (to_x, to_u, to_d, to_s, before, after):
        signal(tm, c)
    barrier = pltpu.get_barrier_semaphore()
    mine = me // per == tm

    @pl.when(mine)
    def _():
        pl.semaphore_wait(barrier, len(targets) + len(origins) + 4)

    @pl.when(jnp.logical_not(mine))
    def _():
        pl.semaphore_wait(barrier, len(targets) + len(origins) + 6)

    def src_copy(t, c, h, send_slot, who):
        return pltpu.make_async_remote_copy(
            src_ref=own_src.at[h * 8 : (h + 1) * 8, :],
            dst_ref=z.at[:, pl.ds(pl.multiple_of(256 + who * n, 128), n)],
            send_sem=src_send.at[send_slot],
            recv_sem=src_recv.at[who],
            device_id=(t, c),
            device_id_type=pl.DeviceIdType.MESH,
        )

    def copy(s_kind, r_kind, c, target, block, half=None, source=None):
        size = ROWS if half is None else ROWS // 2
        start = c * ROWS + (0 if half is None else half * size)
        rows = pl.ds(pl.multiple_of(start, ROWS // 2), size)
        return pltpu.make_async_remote_copy(
            src_ref=rec.at[rows, lanes(block)] if source is None else source.at[rows, :],
            dst_ref=rec.at[rows, lanes(block)],
            send_sem=send.at[s_kind, c],
            recv_sem=recv.at[r_kind, c],
            device_id=(tm, target),
            device_id_type=pl.DeviceIdType.MESH,
        )

    blk_p, blk_u, blk_d = at(y, 1 - x, core), at(up, x, core), at(down, x, core)
    blk_up, blk_dp = at(up, 1 - x, core), at(down, 1 - x, core)
    blk_f, blk_fp = at(far, x, core), at(far, 1 - x, core)

    def sends(c, name):
        table = {
            "own": [
                (0, 0, c, to_x, me, None, wh),
                (1, 2, c, to_u, me, None, wh),
                (2, 1, c, to_d, me, None, wh),
                (3, 8, c, to_s, me, None, wh),
            ],
            "p": [(4, 4, c, to_u, blk_p), (5, 3, c, to_d, blk_p), (6, 9, c, to_s, blk_p)],
            "u": [(7, 6, c, to_d, blk_u, 1), (8, 10, c, to_s, blk_u)],
            "d": [(9, 5, c, to_u, blk_d, 0), (10, 11, c, to_s, blk_d)],
            "f": [(11, 7, c, to_x, blk_f), (12, 14, c, to_s, blk_f)],
            "up": [(13, 12, c, to_s, blk_up)],
            "dp": [(14, 13, c, to_s, blk_dp)],
            "fp": [(15, 15, c, to_s, blk_fp)],
        }
        return [copy(*one) for one in table[name]]

    def start(c, *names):
        for name in names:
            for one in sends(c, name):
                one.start()

    def arrived(c, r_kind, block, half=None):
        copy(0, r_kind, c, to_x, block, half=half).wait_recv()

    tables = ((t_hi, t_mid, t_lo), weight, fwd, inv, band, mean)
    has_left, has_right = me > 0, me < n_chan - 1
    last_lanes, first_lanes = pl.ds(n - LANES, LANES), pl.ds(0, LANES)

    def halo_to_right(source, target, c):
        return pltpu.make_async_remote_copy(
            src_ref=source, dst_ref=target, send_sem=halo_send.at[0, c], recv_sem=halo_recv.at[0, c],
            device_id=(tm, after), device_id_type=pl.DeviceIdType.MESH,
        )

    def halo_to_left(source, target, c):
        return pltpu.make_async_remote_copy(
            src_ref=source, dst_ref=target, send_sem=halo_send.at[1, c], recv_sem=halo_recv.at[1, c],
            device_id=(tm, before), device_id_type=pl.DeviceIdType.MESH,
        )

    def step_rows(c):
        return pl.ds(pl.multiple_of(c * ROWS, ROWS), ROWS)

    def halo_pair(c):
        rows = step_rows(c)
        return (
            halo_to_right(raw.at[rows, last_lanes], left.at[rows, :], c),
            halo_to_left(raw.at[rows, first_lanes], right.at[rows, :], c),
        )

    few_pair = (
        halo_to_right(few.at[:, last_lanes], few_left, steps),
        halo_to_left(few.at[:, first_lanes], few_right, steps),
    )

    def on_sides(pair, name, flip=False):
        sides = (has_left, has_right) if flip else (has_right, has_left)
        for one, there in zip(pair, sides):
            pl.when(there)(getattr(one, name))

    def own_copy(c):
        return pltpu.make_async_copy(wh.at[step_rows(c), :], rec.at[step_rows(c), lanes(me)], own_sem.at[c])

    def whiten_step(c):
        rows = step_rows(c)
        on_sides(halo_pair(c), "wait_recv", flip=True)
        wh[rows, :] = whiten_rows(left[rows, :], raw[rows, :], right[rows, :], ext, *tables)
        start(c, "own")
        own_copy(c).start()

    raw_copy.wait()
    stride = count * n_tm // (8 * n_chan)
    for k in range(8 * per):
        few[k : k + 1, :] = raw[k * stride : k * stride + 1, :]
    on_sides(few_pair, "start")
    for c in range(min(HALOS_AHEAD, steps)):
        on_sides(halo_pair(c), "start")

    @pl.when(me == 0)
    def _():
        left[...] = jnp.zeros(left.shape, F32)
        few_left[...] = jnp.zeros(few_left.shape, F32)

    @pl.when(me == n_chan - 1)
    def _():
        right[...] = jnp.zeros(right.shape, F32)
        few_right[...] = jnp.zeros(few_right.shape, F32)

    bins = spectral.shape[1]
    weight[:, :bins] = spectral[...]
    weight[:, bins:] = spectral[...]
    mean[...] = jnp.full(mean.shape, 1.0 / (2 * bins), BF)
    ext[0:8, :] = jnp.zeros((8, ext.shape[1]), F32)
    ext[0:1, 0 : taps.shape[1]] = taps[...]
    rolled = pltpu.roll(jnp.broadcast_to(ext[0:1, 0:384], (256, 384)), 0, 1, stride=1, stride_axis=0)
    hi, mid, lo = split3(rolled.T)
    t_hi[...] = hi
    t_mid[...] = mid
    t_lo[...] = lo
    ext[...] = jnp.zeros(ext.shape, F32)
    z[:, 0:256] = jnp.zeros((8, 256), F32)
    z[:, 256 + total :] = jnp.zeros((8, 128), F32)
    on_sides(few_pair, "wait_recv", flip=True)
    own_src[...] = whiten_rows(few_left[...], few[...], few_right[...], ext, *tables).astype(F32)

    for slot, (t, c) in enumerate(targets):

        @pl.when((t != tm) | (c != me))
        def _():
            src_copy(t, c, slot % per, slot, me).start()

    @pl.when(mine)
    def _():
        z[:, pl.ds(pl.multiple_of(256 + me * n, 128), n)] = own_src[pl.ds(pl.multiple_of((me % per) * 8, 8), 8), :]

    @pl.loop(0, min(AHEAD, steps))
    def _(c):
        whiten_step(c)

    def lag_part(part, parts):
        @pl.when(part == 0)
        def _():
            for c in range(n_chan):

                @pl.when((me // per != tm) | (c != me))
                def _():
                    src_copy(tm, to_x, 0, 0, c).wait_recv()

        build_lags(z, lagged, total, part, parts)

    scale = total**-0.5
    used = LAGS * 8
    step = -(-used // PIECES // 16) * 16

    def out_copy(c):
        return pltpu.make_async_copy(
            stage.at[c % 2], out.at[:, :, pl.ds(pl.multiple_of(c * COLS, 128), COLS)], out_sem.at[c % 2]
        )

    def partial(c, i, groups):
        first = i * step
        rows = min(step, used - first)
        full = -(-rows // 16) * 16
        acc = None
        for group in groups:
            span = pl.ds(pl.multiple_of(group * (4 * n), 128), 4 * n)
            term = lax.dot_general(
                lagged[first : first + full, span],
                rec[pl.ds(pl.multiple_of(c * COLS, 128), COLS), span],
                (((1,), (1,)), ((), ())),
                preferred_element_type=F32,
            )
            acc = term if acc is None else acc + term
        return slice(first // 8, (first + rows) // 8), acc[:rows].reshape(rows // 8, 8, COLS)

    def near_piece(c, i):
        where, acc = partial(c, i, (y, up, down))
        stage[c % 2, where] = acc

    def far_piece(c, i):
        where, acc = partial(c, i, (far,))
        stage[c % 2, where] = (stage[c % 2, where] + acc) * scale

    def near(c):
        @pl.when(c < steps)
        def _():
            @pl.when(c + HALOS_AHEAD < steps)
            def _():
                on_sides(halo_pair(c + HALOS_AHEAD), "start")

            @pl.when(c + AHEAD < steps)
            def _():
                whiten_step(c + AHEAD)

            arrived(c, 0, blk_p)
            start(c, "p")

    def ring(c):
        @pl.when(c < steps)
        def _():
            arrived(c, 1, blk_u)
            start(c, "u")
            arrived(c, 2, blk_d)
            start(c, "d")

        @pl.when((c >= 1) & (c <= steps))
        def _():
            arrived(c - 1, 5, blk_f, half=0)
            arrived(c - 1, 6, blk_f, half=1)
            start(c - 1, "f")

    def last(c):
        @pl.when((c >= 1) & (c <= steps))
        def _():
            arrived(c - 1, 3, blk_up)
            start(c - 1, "up")
            arrived(c - 1, 4, blk_dp)
            start(c - 1, "dp")

        @pl.when((c >= 2) & (c <= steps + 1))
        def _():
            arrived(c - 2, 7, blk_fp)
            start(c - 2, "fp")

    def twin(c, kinds):
        for kind in kinds:
            yy = {8: y, 9: y, 10: up, 11: down, 12: up, 13: down, 14: far, 15: far}[kind]
            xx = x if kind in (8, 10, 11, 14) else 1 - x
            arrived(c, kind, at(yy, xx, 1 - core))

    @pl.loop(0, chunks + 2)
    def _(m):
        near(2 * m)

        @pl.when(m < 2)
        def _():
            lag_part(2 * m, 4)

        ring(2 * m)

        @pl.when(m >= 2)
        def _():
            b = m - 2
            twin(2 * b, (14, 15))
            twin(2 * b + 1, (14, 15))
            for i in range(PIECES):
                far_piece(b, i)
            out_copy(b).start()

        last(2 * m)
        near(2 * m + 1)

        @pl.when(m < 2)
        def _():
            lag_part(2 * m + 1, 4)

        ready = (m >= 1) & (m <= chunks)

        @pl.when(ready)
        def _():
            b = m - 1
            for c in (2 * b, 2 * b + 1):
                twin(c, (8, 9, 10, 11, 12, 13))
                own_copy(c).wait()

            @pl.when(b >= 2)
            def _():
                out_copy(b - 2).wait()

            near_piece(b, 0)
            near_piece(b, 1)

        ring(2 * m + 1)

        @pl.when(ready)
        def _():
            near_piece(m - 1, 2)
            near_piece(m - 1, 3)

        last(2 * m + 1)

    @pl.loop(0, steps)
    def _(c):
        for name in ("own", "p", "u", "d", "f", "up", "dp", "fp"):
            for one in sends(c, name):
                one.wait_send()

        on_sides(halo_pair(c), "wait_send")

    on_sides(few_pair, "wait_send")
    for slot, (t, c) in enumerate(targets):

        @pl.when((t != tm) | (c != me))
        def _():
            src_copy(t, c, slot % per, slot, me).wait_send()

    out_copy(chunks - 2).wait()
    out_copy(chunks - 1).wait()


def shards(raw_data, fir_taps, spectral_weight):
    count, n = raw_data.shape
    n_tm, n_chan = lax.axis_size("tm"), lax.axis_size("chan")
    total = n * n_chan
    steps = count // ROWS
    few = 8 * n_chan // n_tm
    consts = [jnp.asarray(t) for t in tables()]
    dma = pltpu.SemaphoreType.DMA
    vmem = pl.BlockSpec(memory_space=pltpu.VMEM)
    hbm = pl.BlockSpec(memory_space=pl.ANY)
    result = pl.pallas_call(
        corr_kernel,
        in_specs=[hbm] + [vmem] * 5,
        out_specs=hbm,
        out_shape=jax.ShapeDtypeStruct((LAGS, 8, count), F32),
        scratch_shapes=[
            pltpu.VMEM((count, total), BF),
            pltpu.VMEM(((LAGS + 1) * 8, total), BF),
            pltpu.VMEM((8, total + 384), F32),
            pltpu.VMEM((2, LAGS, 8, COLS), F32),
            pltpu.VMEM((count, n), F32),
            pltpu.VMEM((count, n), BF),
            pltpu.VMEM((few, n), F32),
            pltpu.VMEM((ROWS, 640), F32),
            pltpu.VMEM((count, LANES), F32),
            pltpu.VMEM((count, LANES), F32),
            pltpu.VMEM((few, n), F32),
            pltpu.VMEM((few, LANES), F32),
            pltpu.VMEM((few, LANES), F32),
            pltpu.VMEM((384, 256), BF),
            pltpu.VMEM((384, 256), BF),
            pltpu.VMEM((384, 256), BF),
            pltpu.VMEM((1, SEG), F32),
            pltpu.VMEM((256, SEG), BF),
            dma(()),
            dma((steps,)),
            dma((16, steps)),
            dma((16, steps)),
            dma((n_tm * (n_chan // n_tm),)),
            dma((n_chan,)),
            dma((2,)),
            dma((2, steps + 1)),
            dma((2, steps + 1)),
        ],
        compiler_params=pltpu.CompilerParams(
            collective_id=0, has_side_effects=True, vmem_limit_bytes=60 << 20
        ),
        name="corr",
    )(raw_data, fir_taps[None, :], spectral_weight[None, :], *consts)
    return result.transpose(1, 0, 2)


def solution(mesh):
    in_specs = (P("tm", "chan"), P(), P())
    out_specs = P("chan", None, "tm")
    return jax.shard_map(shards, mesh=mesh, in_specs=in_specs, out_specs=out_specs, check_vma=False)
```

```python
import jax
import jax.numpy as jnp
import ml_dtypes
import numpy as np
from jax import lax
from jax.experimental import pallas as pl
from jax.experimental.pallas import tpu as pltpu
from jax.sharding import PartitionSpec as P

HK = 16
TN = 64
SEG = 128
HALF = 100
LAGS = 201
EPS = 1e-06
FLOOR = 0.5
HALO = HK + TN
BF = jnp.bfloat16
F32 = jnp.float32


def split_np(table):
    table = np.asarray(table, np.float32)
    hi = table.astype(ml_dtypes.bfloat16)
    lo = (table - hi.astype(np.float32)).astype(ml_dtypes.bfloat16)
    return hi, lo


def tables():
    t, f = np.arange(SEG), np.arange(SEG // 2)
    angle = 2.0 * np.pi * ((t[:, None] * f[None, :]) % SEG) / SEG
    forward = np.concatenate([np.cos(angle), np.sin(angle)], axis=1)
    weight = np.where(f == 0, 1.0, 2.0)[:, None]
    inverse = np.concatenate([np.cos(angle).T * weight, np.sin(angle).T * weight]) / np.sqrt(SEG)
    stacked = []
    for table in (forward, inverse):
        row = np.concatenate(split_np(table), axis=1)
        stacked.append(np.concatenate([row, row], axis=0))
    i, o = np.arange(384)[:, None], np.arange(256)[None, :]
    band = ((i - o >= 0) & (i - o <= 2 * TN)).astype(ml_dtypes.bfloat16)
    return stacked[0], stacked[1], band


def dot(a, b):
    return jnp.dot(a, b, preferred_element_type=F32)


def split2(x):
    hi = x.astype(BF)
    return hi, (x - hi.astype(F32)).astype(BF)


def split3(x):
    hi = x.astype(BF)
    rest = x - hi.astype(F32)
    mid = rest.astype(BF)
    return hi, mid, (rest - mid.astype(F32)).astype(BF)


def whiten_rows(left, raw, right, ext, taps, weight, fwd, inv, band, mean):
    rows, n = raw.shape
    here = pl.ds(0, rows)
    chan, ends = lax.axis_index("chan"), lax.axis_size("chan") - 1
    ext[here, 0:HALO] = left[:, left.shape[1] - HALO :]
    ext[here, HALO : HALO + n] = raw
    ext[here, HALO + n : 2 * HALO + n] = right[:, :HALO]
    t_hi, t_mid, t_lo = taps

    def fir(x):
        hi, mid, lo = split3(x)
        small = dot(mid, t_mid[...]) + dot(hi, t_lo[...]) + dot(lo, t_hi[...])
        return (small + (dot(hi, t_mid[...]) + dot(mid, t_hi[...]))) + dot(hi, t_hi[...])

    f = jnp.concatenate([fir(ext[here, 0:384]), fir(ext[here, 256:640])], axis=1)
    lane = lax.broadcasted_iota(jnp.int32, (1, 512), 1)
    low = jnp.where(chan == 0, TN, 0)
    high = jnp.where(chan == ends, TN + n, 512)
    f = jnp.where((lane >= low) & (lane < high), f, 0.0)
    hi, lo = split2(jnp.abs(f))
    first = dot(hi[:, 0:384], band[...]) + dot(lo[:, 0:384], band[...])
    second = dot(hi[:, 256:512], band[0:256, 0:128]) + dot(lo[:, 256:512], band[0:256, 0:128])
    summed = jnp.concatenate([first, second], axis=1)
    norm = f[:, TN : TN + n] / (summed * (1.0 / (2 * TN + 1)) + EPS)
    parts = []
    for s in range(n // SEG):
        x = norm[:, s * SEG : (s + 1) * SEG]
        p = dot(jnp.concatenate(split2(x), axis=1), fwd[...])
        spec = p[:, :SEG] + p[:, SEG:]
        sq = spec * spec
        amp = jnp.sqrt(sq + pltpu.roll(sq, SEG // 2, 1))
        mean_amp = dot(jnp.concatenate(split2(amp), axis=1), mean[...]) + EPS
        z = spec * (weight[...] / jnp.maximum(amp, FLOOR * mean_amp))
        q = dot(jnp.concatenate(split2(z), axis=1), inv[...])
        parts.append((q[:, :SEG] + q[:, SEG:]).astype(BF))
    return jnp.concatenate(parts, axis=1)


AHEAD = 4
HALOS_AHEAD = 6
LANES = 128
COLS = 256
ROWS = 128
PIECES = 4


def build_lags(z, lagged, total, part, parts):
    lane = lax.broadcasted_iota(jnp.int32, (8, 128), 1)
    blocks = total // 128

    @pl.loop(part * (64 // parts), (part + 1) * (64 // parts))
    def _(p):
        shift = p * 2
        tiles = []
        for one in (shift, shift + 1):
            rolled = [pltpu.roll(z[:, j * 128 : (j + 1) * 128], one, 1) for j in range(1, blocks + 3)]
            tiles.append([jnp.where(lane < one, rolled[j], rolled[j + 1]) for j in range(blocks + 1)])
        pairs = [jnp.concatenate([tiles[0][j], tiles[1][j]], axis=0).astype(BF) for j in range(blocks + 1)]

        @pl.when(shift + HALF < LAGS)
        def _():
            row = pl.ds(pl.multiple_of((shift + HALF) * 8, 16), 16)
            for j in range(blocks):
                lagged[row, j * 128 : (j + 1) * 128] = pairs[j]

        @pl.when(shift >= 128 - HALF)
        def _():
            row = pl.ds(pl.multiple_of((shift - (128 - HALF)) * 8, 16), 16)
            for j in range(blocks):
                lagged[row, j * 128 : (j + 1) * 128] = pairs[j + 1]


def corr_kernel(
    raw_hbm, taps, spectral, fwd, inv, band, out,
    rec, lagged, z, stage, raw, wh, own_src, ext, left, right, few, few_left, few_right, t_hi, t_mid, t_lo, weight, mean,
    raw_sem, own_sem, send, recv, src_send, src_recv, out_sem, halo_send, halo_recv,
):
    tm, me = lax.axis_index("tm"), lax.axis_index("chan")
    n_tm, n_chan = lax.axis_size("tm"), lax.axis_size("chan")
    count, n = wh.shape
    total = n * n_chan
    chunks, steps = count // COLS, count // ROWS
    y, x, core = me // 4, (me // 2) % 2, me % 2
    n_y = n_chan // 4
    up, down, far = (y + 1) % n_y, (y + n_y - 1) % n_y, (y + 2) % n_y

    def at(yy, xx, cc):
        return (yy * 2 + xx) * 2 + cc

    raw_copy = pltpu.make_async_copy(raw_hbm, raw, raw_sem)
    raw_copy.start()
    to_x, to_u, to_d, to_s = at(y, 1 - x, core), at(up, x, core), at(down, x, core), at(y, x, 1 - core)

    def lanes(b):
        return pl.ds(pl.multiple_of(b * n, 128), n)

    def signal(t, c):
        pl.semaphore_signal(
            pltpu.get_barrier_semaphore(), inc=1, device_id=(t, c), device_id_type=pl.DeviceIdType.MESH
        )

    per = n_chan // n_tm
    targets = [(t, per * tm + h) for t in range(n_tm) for h in range(per)]
    origins = [(me // per, c) for c in range(n_chan)]
    for t, c in targets + origins:

        @pl.when((t != tm) | (c != me))
        def _():
            signal(t, c)

    before, after = (me + n_chan - 1) % n_chan, (me + 1) % n_chan
    for c in (to_x, to_u, to_d, to_s, before, after):
        signal(tm, c)
    barrier = pltpu.get_barrier_semaphore()
    mine = me // per == tm

    @pl.when(mine)
    def _():
        pl.semaphore_wait(barrier, len(targets) + len(origins) + 4)

    @pl.when(jnp.logical_not(mine))
    def _():
        pl.semaphore_wait(barrier, len(targets) + len(origins) + 6)

    def src_copy(t, c, h, send_slot, who):
        return pltpu.make_async_remote_copy(
            src_ref=own_src.at[h * 8 : (h + 1) * 8, :],
            dst_ref=z.at[:, pl.ds(pl.multiple_of(256 + who * n, 128), n)],
            send_sem=src_send.at[send_slot],
            recv_sem=src_recv.at[who],
            device_id=(t, c),
            device_id_type=pl.DeviceIdType.MESH,
        )

    def copy(s_kind, r_kind, c, target, block, half=None, source=None):
        size = ROWS if half is None else ROWS // 2
        start = c * ROWS + (0 if half is None else half * size)
        rows = pl.ds(pl.multiple_of(start, ROWS // 2), size)
        return pltpu.make_async_remote_copy(
            src_ref=rec.at[rows, lanes(block)] if source is None else source.at[rows, :],
            dst_ref=rec.at[rows, lanes(block)],
            send_sem=send.at[s_kind, c],
            recv_sem=recv.at[r_kind, c],
            device_id=(tm, target),
            device_id_type=pl.DeviceIdType.MESH,
        )

    blk_p, blk_u, blk_d = at(y, 1 - x, core), at(up, x, core), at(down, x, core)
    blk_up, blk_dp = at(up, 1 - x, core), at(down, 1 - x, core)
    blk_f, blk_fp = at(far, x, core), at(far, 1 - x, core)

    def sends(c, name):
        table = {
            "own": [
                (0, 0, c, to_x, me, None, wh),
                (1, 2, c, to_u, me, None, wh),
                (2, 1, c, to_d, me, None, wh),
                (3, 8, c, to_s, me, None, wh),
            ],
            "p": [(4, 4, c, to_u, blk_p), (5, 3, c, to_d, blk_p), (6, 9, c, to_s, blk_p)],
            "u": [(7, 6, c, to_d, blk_u, 1), (8, 10, c, to_s, blk_u)],
            "d": [(9, 5, c, to_u, blk_d, 0), (10, 11, c, to_s, blk_d)],
            "f": [(11, 7, c, to_x, blk_f), (12, 14, c, to_s, blk_f)],
            "up": [(13, 12, c, to_s, blk_up)],
            "dp": [(14, 13, c, to_s, blk_dp)],
            "fp": [(15, 15, c, to_s, blk_fp)],
        }
        return [copy(*one) for one in table[name]]

    def start(c, *names):
        for name in names:
            for one in sends(c, name):
                one.start()

    def arrived(c, r_kind, block, half=None):
        copy(0, r_kind, c, to_x, block, half=half).wait_recv()

    tables = ((t_hi, t_mid, t_lo), weight, fwd, inv, band, mean)
    has_left, has_right = me > 0, me < n_chan - 1
    last_lanes, first_lanes = pl.ds(n - LANES, LANES), pl.ds(0, LANES)

    def halo_to_right(source, target, c):
        return pltpu.make_async_remote_copy(
            src_ref=source, dst_ref=target, send_sem=halo_send.at[0, c], recv_sem=halo_recv.at[0, c],
            device_id=(tm, after), device_id_type=pl.DeviceIdType.MESH,
        )

    def halo_to_left(source, target, c):
        return pltpu.make_async_remote_copy(
            src_ref=source, dst_ref=target, send_sem=halo_send.at[1, c], recv_sem=halo_recv.at[1, c],
            device_id=(tm, before), device_id_type=pl.DeviceIdType.MESH,
        )

    def step_rows(c):
        return pl.ds(pl.multiple_of(c * ROWS, ROWS), ROWS)

    def halo_pair(c):
        rows = step_rows(c)
        return (
            halo_to_right(raw.at[rows, last_lanes], left.at[rows, :], c),
            halo_to_left(raw.at[rows, first_lanes], right.at[rows, :], c),
        )

    few_pair = (
        halo_to_right(few.at[:, last_lanes], few_left, steps),
        halo_to_left(few.at[:, first_lanes], few_right, steps),
    )

    def on_sides(pair, name, flip=False):
        sides = (has_left, has_right) if flip else (has_right, has_left)
        for one, there in zip(pair, sides):
            pl.when(there)(getattr(one, name))

    def own_copy(c):
        return pltpu.make_async_copy(wh.at[step_rows(c), :], rec.at[step_rows(c), lanes(me)], own_sem.at[c])

    def whiten_step(c):
        rows = step_rows(c)
        on_sides(halo_pair(c), "wait_recv", flip=True)
        wh[rows, :] = whiten_rows(left[rows, :], raw[rows, :], right[rows, :], ext, *tables)
        start(c, "own")
        own_copy(c).start()

    raw_copy.wait()
    stride = count * n_tm // (8 * n_chan)
    for k in range(8 * per):
        few[k : k + 1, :] = raw[k * stride : k * stride + 1, :]
    on_sides(few_pair, "start")
    for c in range(min(HALOS_AHEAD, steps)):
        on_sides(halo_pair(c), "start")

    @pl.when(me == 0)
    def _():
        left[...] = jnp.zeros(left.shape, F32)
        few_left[...] = jnp.zeros(few_left.shape, F32)

    @pl.when(me == n_chan - 1)
    def _():
        right[...] = jnp.zeros(right.shape, F32)
        few_right[...] = jnp.zeros(few_right.shape, F32)

    bins = spectral.shape[1]
    weight[:, :bins] = spectral[...]
    weight[:, bins:] = spectral[...]
    mean[...] = jnp.full(mean.shape, 1.0 / (2 * bins), BF)
    ext[0:8, :] = jnp.zeros((8, ext.shape[1]), F32)
    ext[0:1, 0 : taps.shape[1]] = taps[...]
    rolled = pltpu.roll(jnp.broadcast_to(ext[0:1, 0:384], (256, 384)), 0, 1, stride=1, stride_axis=0)
    hi, mid, lo = split3(rolled.T)
    t_hi[...] = hi
    t_mid[...] = mid
    t_lo[...] = lo
    ext[...] = jnp.zeros(ext.shape, F32)
    z[:, 0:256] = jnp.zeros((8, 256), F32)
    z[:, 256 + total :] = jnp.zeros((8, 128), F32)
    on_sides(few_pair, "wait_recv", flip=True)
    own_src[...] = whiten_rows(few_left[...], few[...], few_right[...], ext, *tables).astype(F32)

    for slot, (t, c) in enumerate(targets):

        @pl.when((t != tm) | (c != me))
        def _():
            src_copy(t, c, slot % per, slot, me).start()

    @pl.when(mine)
    def _():
        z[:, pl.ds(pl.multiple_of(256 + me * n, 128), n)] = own_src[pl.ds(pl.multiple_of((me % per) * 8, 8), 8), :]

    @pl.loop(0, min(AHEAD, steps))
    def _(c):
        whiten_step(c)

    def lag_part(part, parts):
        @pl.when(part == 0)
        def _():
            for c in range(n_chan):

                @pl.when((me // per != tm) | (c != me))
                def _():
                    src_copy(tm, to_x, 0, 0, c).wait_recv()

        build_lags(z, lagged, total, part, parts)

    scale = total**-0.5
    used = LAGS * 8
    step = -(-used // PIECES // 16) * 16

    def out_copy(c):
        return pltpu.make_async_copy(
            stage.at[c % 2], out.at[:, :, pl.ds(pl.multiple_of(c * COLS, 128), COLS)], out_sem.at[c % 2]
        )

    def partial(c, i, groups):
        first = i * step
        rows = min(step, used - first)
        full = -(-rows // 16) * 16
        acc = None
        for group in groups:
            span = pl.ds(pl.multiple_of(group * (4 * n), 128), 4 * n)
            term = lax.dot_general(
                lagged[first : first + full, span],
                rec[pl.ds(pl.multiple_of(c * COLS, 128), COLS), span],
                (((1,), (1,)), ((), ())),
                preferred_element_type=F32,
            )
            acc = term if acc is None else acc + term
        return slice(first // 8, (first + rows) // 8), acc[:rows].reshape(rows // 8, 8, COLS)

    def near_piece(c, i):
        where, acc = partial(c, i, (y, up, down))
        stage[c % 2, where] = acc

    def far_piece(c, i):
        where, acc = partial(c, i, (far,))
        stage[c % 2, where] = (stage[c % 2, where] + acc) * scale

    def near(c):
        @pl.when(c < steps)
        def _():
            arrived(c, 0, blk_p)
            start(c, "p")

    def ring(c):
        @pl.when(c < steps)
        def _():
            arrived(c, 1, blk_u)
            start(c, "u")
            arrived(c, 2, blk_d)
            start(c, "d")

            @pl.when(c + HALOS_AHEAD < steps)
            def _():
                on_sides(halo_pair(c + HALOS_AHEAD), "start")

            @pl.when(c + AHEAD < steps)
            def _():
                whiten_step(c + AHEAD)

        @pl.when((c >= 1) & (c <= steps))
        def _():
            arrived(c - 1, 5, blk_f, half=0)
            arrived(c - 1, 6, blk_f, half=1)
            start(c - 1, "f")

    def last(c):
        @pl.when((c >= 1) & (c <= steps))
        def _():
            arrived(c - 1, 3, blk_up)
            start(c - 1, "up")
            arrived(c - 1, 4, blk_dp)
            start(c - 1, "dp")

        @pl.when((c >= 2) & (c <= steps + 1))
        def _():
            arrived(c - 2, 7, blk_fp)
            start(c - 2, "fp")

    def twin(c, kinds):
        for kind in kinds:
            yy = {8: y, 9: y, 10: up, 11: down, 12: up, 13: down, 14: far, 15: far}[kind]
            xx = x if kind in (8, 10, 11, 14) else 1 - x
            arrived(c, kind, at(yy, xx, 1 - core))

    @pl.loop(0, chunks + 2)
    def _(m):
        near(2 * m)

        @pl.when(m < 2)
        def _():
            lag_part(2 * m, 4)

        ring(2 * m)

        @pl.when(m >= 2)
        def _():
            b = m - 2
            twin(2 * b, (14, 15))
            twin(2 * b + 1, (14, 15))
            for i in range(PIECES):
                far_piece(b, i)
            out_copy(b).start()

        last(2 * m)
        near(2 * m + 1)

        @pl.when(m < 2)
        def _():
            lag_part(2 * m + 1, 4)

        ready = (m >= 1) & (m <= chunks)

        @pl.when(ready)
        def _():
            b = m - 1
            for c in (2 * b, 2 * b + 1):
                twin(c, (8, 9, 10, 11, 12, 13))
                own_copy(c).wait()

            @pl.when(b >= 2)
            def _():
                out_copy(b - 2).wait()

            near_piece(b, 0)
            near_piece(b, 1)

        ring(2 * m + 1)

        @pl.when(ready)
        def _():
            near_piece(m - 1, 2)
            near_piece(m - 1, 3)

        last(2 * m + 1)

    @pl.loop(0, steps)
    def _(c):
        for name in ("own", "p", "u", "d", "f", "up", "dp", "fp"):
            for one in sends(c, name):
                one.wait_send()

        on_sides(halo_pair(c), "wait_send")

    on_sides(few_pair, "wait_send")
    for slot, (t, c) in enumerate(targets):

        @pl.when((t != tm) | (c != me))
        def _():
            src_copy(t, c, slot % per, slot, me).wait_send()

    out_copy(chunks - 2).wait()
    out_copy(chunks - 1).wait()


def shards(raw_data, fir_taps, spectral_weight):
    count, n = raw_data.shape
    n_tm, n_chan = lax.axis_size("tm"), lax.axis_size("chan")
    total = n * n_chan
    steps = count // ROWS
    few = 8 * n_chan // n_tm
    consts = [jnp.asarray(t) for t in tables()]
    dma = pltpu.SemaphoreType.DMA
    vmem = pl.BlockSpec(memory_space=pltpu.VMEM)
    hbm = pl.BlockSpec(memory_space=pl.ANY)
    result = pl.pallas_call(
        corr_kernel,
        in_specs=[hbm] + [vmem] * 5,
        out_specs=hbm,
        out_shape=jax.ShapeDtypeStruct((LAGS, 8, count), F32),
        scratch_shapes=[
            pltpu.VMEM((count, total), BF),
            pltpu.VMEM(((LAGS + 1) * 8, total), BF),
            pltpu.VMEM((8, total + 384), F32),
            pltpu.VMEM((2, LAGS, 8, COLS), F32),
            pltpu.VMEM((count, n), F32),
            pltpu.VMEM((count, n), BF),
            pltpu.VMEM((few, n), F32),
            pltpu.VMEM((ROWS, 640), F32),
            pltpu.VMEM((count, LANES), F32),
            pltpu.VMEM((count, LANES), F32),
            pltpu.VMEM((few, n), F32),
            pltpu.VMEM((few, LANES), F32),
            pltpu.VMEM((few, LANES), F32),
            pltpu.VMEM((384, 256), BF),
            pltpu.VMEM((384, 256), BF),
            pltpu.VMEM((384, 256), BF),
            pltpu.VMEM((1, SEG), F32),
            pltpu.VMEM((256, SEG), BF),
            dma(()),
            dma((steps,)),
            dma((16, steps)),
            dma((16, steps)),
            dma((n_tm * (n_chan // n_tm),)),
            dma((n_chan,)),
            dma((2,)),
            dma((2, steps + 1)),
            dma((2, steps + 1)),
        ],
        compiler_params=pltpu.CompilerParams(
            collective_id=0, has_side_effects=True, vmem_limit_bytes=60 << 20
        ),
        name="corr",
    )(raw_data, fir_taps[None, :], spectral_weight[None, :], *consts)
    return result.transpose(1, 0, 2)


def solution(mesh):
    in_specs = (P("tm", "chan"), P(), P())
    out_specs = P("chan", None, "tm")
    return jax.shard_map(shards, mesh=mesh, in_specs=in_specs, out_specs=out_specs, check_vma=False)
```
